32 devices in a mesh: grp: 8 (over z, y), tp: 2 (over core), fs: 2 (over x).
Axes of the slice: x: 2, y: 2, z: 4, core: 2. Of those that a mesh axis runs over, the one named last changes fastest.
Arguments:
- tokens: bfloat16 [512, 4, 8192], P('grp', None, ('tp', 'fs')), may hold values from -64 to 64
- norm_gain: bfloat16 [8192], P(('tp', 'fs')), may hold values from 0.25 to 1.75
- queries: bfloat16 [512, 4, 8192], P('grp', None, ('tp', 'fs')), may hold values from -64 to 64
- rotated_key_cache: bfloat16 [512, 32, 1024], P('grp', None, ('tp', 'fs')), may hold values from -6 to 6
- head_value_cache: bfloat16 [512, 32, 1024], P('grp', None, ('tp', 'fs')), may hold values from -6 to 6
- lengths: int32 [512], P('grp'), may hold values from 2 to 32
- master: float32 [8192, 2048], P('grp', ('tp', 'fs')), may hold values from -0.0625 to 0.0625
- moment_first: float32 [8192, 2048], P('grp', ('tp', 'fs')), may hold values from -4 to 4
- moment_second: float32 [8192, 2048], P('grp', ('tp', 'fs')), may hold values from 0.1 to 1
- gradient: float32 [8192, 2048], P('grp', ('tp', 'fs')), may hold values from -6 to 6
Outputs:
- attended: bfloat16 [512, 4, 8192], P('grp', None, ('tp', 'fs'))
- appended: bfloat16 [512, 4, 2048], P('grp', None, ('tp', 'fs'))
- new_master: float32 [8192, 2048], P('grp', ('tp', 'fs'))
- new_first: float32 [8192, 2048], P('grp', ('tp', 'fs'))
- new_second: float32 [8192, 2048], P('grp', ('tp', 'fs'))
The draws below stay inside these ranges and needn't reach their ends.
All inputs are finite; a program needn't handle non-finite values.
Results may differ from the reference program's by a relative error of at most 0.0057.
Values may be sent and summed in bfloat16 or wider, within the bound.
A program may use at most 128 MiB of HBM per device.

```python
import math
import jax
import jax.numpy as jnp
from jax import lax

MODEL_WIDTH = 8192
QUERY_HEADS = 64
KEY_VALUE_HEADS = 8
HEAD_SIZE = 128
REPLICA_ROWS = 64
CACHE_SLOTS = 32
NEW_TOKENS = 4
TOTAL_ROWS = 512
KV_COLS = 2048
N_GRP = 8


def drawn_draw(key):
    cache_seed = jax.random.fold_in(key, 7001)
    query_seed = jax.random.fold_in(key, 7002)
    cache_dimensions = (TOTAL_ROWS, CACHE_SLOTS, KEY_VALUE_HEADS * HEAD_SIZE)
    query_shape = (TOTAL_ROWS, NEW_TOKENS, QUERY_HEADS * HEAD_SIZE)
    cache_key_seeds = jnp.clip(jax.random.normal(cache_seed, cache_dimensions, jnp.float32), -6.0, 6.0)
    query_draw = jnp.clip(jax.random.normal(query_seed, query_shape, jnp.float32), -6.0, 6.0)
    return (cache_key_seeds, query_draw)


def draw_rotated_key_cache(key, part):
    return drawn_draw(key)[0].astype(jnp.bfloat16)


def draw_queries(key, part):
    return drawn_draw(key)[1].astype(jnp.bfloat16)


def draw_tokens(key, part):
    base_seed = jax.random.fold_in(key, 8001)
    shape = (TOTAL_ROWS, NEW_TOKENS, MODEL_WIDTH)
    values = jnp.clip(jax.random.normal(base_seed, shape, jnp.float32), -6.0, 6.0)
    return values.astype(jnp.bfloat16)


def place_ends(result, stream_key, low, high):
    longest = result.shape.index(max(result.shape))
    spots = []
    for shift in (0, 1):
        where = [jax.random.randint(jax.random.fold_in(stream_key, axis), (), 0, length) for axis, length in enumerate(result.shape)]
        where[longest] = (where[longest] + shift) % result.shape[longest]
        spots.append(tuple(where))
    return result.at[spots[0]].set(low).at[spots[1]].set(high)


def block_levels(stream_key, shape, cuts, low, largest):
    def one(axis_at, blocks):
        steps = jax.random.uniform(jax.random.fold_in(jax.random.fold_in(stream_key, 6), axis_at), (blocks,), jnp.float32, low / len(cuts), largest / len(cuts))
        return jnp.repeat(jnp.exp(steps), shape[axis_at] // blocks).reshape((-1,) + (1,) * (len(shape) - axis_at - 1))

    factor_of = one(*cuts[0])
    for cut in cuts[1:]:
        factor_of = factor_of * one(*cut)
    return factor_of


def noise(key, shape, scale, limit, cuts=(), held_as=jnp.bfloat16):
    factor_of = block_levels(key, shape, cuts, -0.22, 0.18) if cuts else 1.0
    result = jax.random.normal(key, shape, jnp.float32) * scale * factor_of
    return jnp.minimum(jnp.maximum(result, -limit), limit).astype(held_as)


def setup_inputs(seed: int = 0) -> dict:
    splits = jax.random.split(jax.random.key(seed), 11)
    return {
        "tokens": draw_tokens(jax.random.fold_in(splits[10], 71), 0),
        "norm_gain": jnp.clip(1.0 + 0.15 * jax.random.normal(splits[1], (MODEL_WIDTH,), jnp.float32), 0.25, 1.75).astype(jnp.bfloat16),
        "queries": draw_queries(jax.random.fold_in(splits[10], 71), 0),
        "rotated_key_cache": draw_rotated_key_cache(jax.random.fold_in(splits[10], 71), 0),
        "head_value_cache": noise(splits[4], (TOTAL_ROWS, CACHE_SLOTS, KEY_VALUE_HEADS * HEAD_SIZE), 1.0, 6.0, ((0, 8), (2, 4))),
        "lengths": place_ends(jax.random.randint(splits[5], (TOTAL_ROWS,), 2, CACHE_SLOTS + 1), jax.random.fold_in(splits[5], 1), 2, CACHE_SLOTS).astype(jnp.int32),
        "master": noise(splits[6], (MODEL_WIDTH, KV_COLS), MODEL_WIDTH ** -0.5, 0.0625, ((0, 8), (1, 4)), jnp.float32),
        "moment_first": noise(splits[7], (MODEL_WIDTH, KV_COLS), 0.3, 4.0, ((0, 8), (1, 4)), jnp.float32),
        "moment_second": jnp.clip(jnp.exp(math.log(1.0) - 2.3025851 * jax.random.uniform(splits[8], (MODEL_WIDTH, KV_COLS), jnp.float32) ** block_levels(splits[8], (MODEL_WIDTH, KV_COLS), ((0, 8), (1, 4)), -0.2, 0.2)), 0.1, 1.0),
        "gradient": noise(splits[9], (MODEL_WIDTH, KV_COLS), 1.0, 6.0, ((0, 8), (1, 4)), jnp.float32),
    }


beta_first = 0.9
beta_second = 0.999
correct_first = 0.9999734386011124
correct_second = 0.09520785288629038
adam_eps = 1e-08
learn_rate = 0.003
decay_rate = 0.1
norm_eps = 1e-06
rope_base = 1000000.0

def rotate(keys, positions):
    halfway = keys.shape[-1] // 2
    frequency = rope_base ** (-(jnp.arange(halfway, dtype=jnp.float32) * 2.0 / keys.shape[-1]))
    angles = positions[:, :, None] * frequency[None, None, :]
    cosine = jnp.cos(angles)[:, :, None, :]
    sine = jnp.sin(angles)[:, :, None, :]
    first_half = keys[..., :halfway]
    second_half = keys[..., halfway:]
    return jnp.concatenate([first_half * cosine - second_half * sine, second_half * cosine + first_half * sine], axis=-1)

def attention(queries, rotated_key_cache, head_value_cache, key_new, value_new, lengths):
    batch_rows, steps = (queries.shape[0], queries.shape[1])
    window = rotated_key_cache.shape[1]
    kv_heads = rotated_key_cache.shape[2] // HEAD_SIZE
    sharing_factor = QUERY_HEADS // KEY_VALUE_HEADS
    factor = HEAD_SIZE ** (-0.5)
    query_heads = queries.reshape(batch_rows, steps, kv_heads, sharing_factor, HEAD_SIZE).astype(jnp.float32)
    cache_key_seeds = rotated_key_cache.reshape(batch_rows, window, kv_heads, HEAD_SIZE).astype(jnp.float32)
    cache_values = head_value_cache.reshape(batch_rows, window, kv_heads, HEAD_SIZE).astype(jnp.float32)
    scores_cached = jnp.einsum('rsxgd,rlxd->rxgsl', query_heads, cache_key_seeds) * factor
    scores_fresh = jnp.einsum('rsxgd,ruxd->rxgsu', query_heads, key_new.astype(jnp.float32)) * factor
    present = (jnp.arange(window, dtype=jnp.int32)[None, :] < lengths[:, None])[:, None, None, None, :]
    causal = (jnp.arange(steps, dtype=jnp.int32)[None, :] <= jnp.arange(steps, dtype=jnp.int32)[:, None])[None, None, None, :, :]
    scores_cached = jnp.where(present, scores_cached, -jnp.inf)
    scores_fresh = jnp.where(causal, scores_fresh, -jnp.inf)
    ceiling = jnp.maximum(lax.optimization_barrier(jnp.max(scores_cached, axis=-1, keepdims=True)), lax.optimization_barrier(jnp.max(scores_fresh, axis=-1, keepdims=True)))
    probs_cached = jnp.exp(scores_cached - ceiling)
    probs_fresh = jnp.exp(scores_fresh - ceiling)
    denom = lax.optimization_barrier(jnp.sum(probs_cached, axis=-1, keepdims=True)) + lax.optimization_barrier(jnp.sum(probs_fresh, axis=-1, keepdims=True))
    weights_cached = probs_cached.astype(jnp.bfloat16).astype(jnp.float32)
    weights_fresh = probs_fresh.astype(jnp.bfloat16).astype(jnp.float32)
    blended = jnp.einsum('rxgsl,rlxd->rsxgd', weights_cached, cache_values)
    blended = blended + jnp.einsum('rxgsu,ruxd->rsxgd', weights_fresh, value_new.astype(jnp.float32))
    blended = blended / jnp.transpose(denom, (0, 3, 1, 2, 4))
    return blended.astype(jnp.bfloat16).reshape(batch_rows, steps, kv_heads * sharing_factor * HEAD_SIZE)

def reference(tokens, norm_gain, queries, rotated_key_cache, head_value_cache, lengths, master, moment_first, moment_second, gradient):
    average = beta_first * moment_first + (1.0 - beta_first) * gradient
    variance = beta_second * moment_second + (1.0 - beta_second) * gradient * gradient
    update = average / correct_first / (jnp.sqrt(variance / correct_second) + adam_eps)
    renewed = master - learn_rate * (update + decay_rate * master)
    layer_half = renewed.astype(jnp.bfloat16)
    gain_wide = norm_gain.astype(jnp.float32)

    def replica(bundle):
        replica_tokens, replica_queries, replica_keys, replica_values, replica_lengths = bundle
        widened = replica_tokens.astype(jnp.float32)
        mean_square = lax.optimization_barrier(jnp.sum(widened * widened, axis=-1, keepdims=True)) / MODEL_WIDTH
        normed = (widened * lax.rsqrt(mean_square + norm_eps) * gain_wide).astype(jnp.bfloat16)
        projected_output = jnp.dot(normed.reshape(REPLICA_ROWS * NEW_TOKENS, MODEL_WIDTH), layer_half, preferred_element_type=jnp.float32)
        projected_output = projected_output.reshape(REPLICA_ROWS, NEW_TOKENS, KEY_VALUE_HEADS, 2, HEAD_SIZE)
        positions = (replica_lengths[:, None] + jnp.arange(NEW_TOKENS, dtype=jnp.int32)[None, :]).astype(jnp.float32)
        key_new = rotate(projected_output[:, :, :, 0, :], positions).astype(jnp.bfloat16)
        value_new = projected_output[:, :, :, 1, :].astype(jnp.bfloat16)
        appended = jnp.stack([key_new, value_new], axis=3).reshape(REPLICA_ROWS, NEW_TOKENS, KV_COLS)
        attended = attention(replica_queries, replica_keys, replica_values, key_new, value_new, replica_lengths)
        return (attended, appended)
    grouped_bundles = (tokens.reshape(N_GRP, REPLICA_ROWS, NEW_TOKENS, MODEL_WIDTH), queries.reshape(N_GRP, REPLICA_ROWS, NEW_TOKENS, QUERY_HEADS * HEAD_SIZE), rotated_key_cache.reshape(N_GRP, REPLICA_ROWS, CACHE_SLOTS, KEY_VALUE_HEADS * HEAD_SIZE), head_value_cache.reshape(N_GRP, REPLICA_ROWS, CACHE_SLOTS, KEY_VALUE_HEADS * HEAD_SIZE), lengths.reshape(N_GRP, REPLICA_ROWS))
    attended, appended = lax.map(replica, grouped_bundles)
    attended = attended.reshape(TOTAL_ROWS, NEW_TOKENS, QUERY_HEADS * HEAD_SIZE)
    appended = appended.reshape(TOTAL_ROWS, NEW_TOKENS, KV_COLS)
    return (attended, appended, renewed, average, variance)
```

```python
import functools

import jax
import jax.numpy as jnp
from jax import lax
from jax.experimental import pallas as pl
from jax.experimental.pallas import tpu as pltpu
from jax.sharding import PartitionSpec as P

MESH_ID = pl.DeviceIdType.MESH
PIECES = 2

MODEL_WIDTH = 8192
QUERY_HEADS = 64
KEY_VALUE_HEADS = 8
HEAD_SIZE = 128


beta_first = 0.9
beta_second = 0.999
correct_first = 0.9999734386011124
correct_second = 0.09520785288629038
adam_eps = 1e-08
learn_rate = 0.003
decay_rate = 0.1
norm_eps = 1e-06
rope_base = 1000000.0


def rotate(keys, positions):
    halfway = keys.shape[-1] // 2
    frequency = rope_base ** (-(jnp.arange(halfway, dtype=jnp.float32) * 2.0 / keys.shape[-1]))
    angles = positions[:, :, None] * frequency[None, None, :]
    cosine = jnp.cos(angles)[:, :, None, :]
    sine = jnp.sin(angles)[:, :, None, :]
    first_half = keys[..., :halfway]
    second_half = keys[..., halfway:]
    return jnp.concatenate(
        [first_half * cosine - second_half * sine, second_half * cosine + first_half * sine],
        axis=-1,
    )


def attention(queries, rotated_key_cache, head_value_cache, key_new, value_new, lengths):
    batch_rows, steps = (queries.shape[0], queries.shape[1])
    window = rotated_key_cache.shape[1]
    kv_heads = rotated_key_cache.shape[2] // HEAD_SIZE
    sharing_factor = QUERY_HEADS // KEY_VALUE_HEADS
    factor = HEAD_SIZE ** (-0.5)
    query_heads = queries.reshape(batch_rows, steps, kv_heads, sharing_factor, HEAD_SIZE)
    cache_key_seeds = rotated_key_cache.reshape(batch_rows, window, kv_heads, HEAD_SIZE)
    cache_values = head_value_cache.reshape(batch_rows, window, kv_heads, HEAD_SIZE)
    scores_cached = (
        jnp.einsum(
            "rsxgd,rlxd->rxgsl", query_heads, cache_key_seeds, preferred_element_type=jnp.float32
        )
        * factor
    )
    scores_fresh = (
        jnp.einsum("rsxgd,ruxd->rxgsu", query_heads, key_new, preferred_element_type=jnp.float32)
        * factor
    )
    present = (jnp.arange(window, dtype=jnp.int32)[None, :] < lengths[:, None])[
        :, None, None, None, :
    ]
    causal = (
        jnp.arange(steps, dtype=jnp.int32)[None, :] <= jnp.arange(steps, dtype=jnp.int32)[:, None]
    )[None, None, None, :, :]
    scores_cached = jnp.where(present, scores_cached, -jnp.inf)
    scores_fresh = jnp.where(causal, scores_fresh, -jnp.inf)
    ceiling = jnp.maximum(
        jnp.max(scores_cached, axis=-1, keepdims=True),
        jnp.max(scores_fresh, axis=-1, keepdims=True),
    )
    probs_cached = jnp.exp(scores_cached - ceiling)
    probs_fresh = jnp.exp(scores_fresh - ceiling)
    denom = jnp.sum(probs_cached, axis=-1, keepdims=True) + jnp.sum(
        probs_fresh, axis=-1, keepdims=True
    )
    weights_cached = probs_cached.astype(jnp.bfloat16)
    weights_fresh = probs_fresh.astype(jnp.bfloat16)
    blended = jnp.einsum(
        "rxgsl,rlxd->rsxgd", weights_cached, cache_values, preferred_element_type=jnp.float32
    )
    blended = blended + jnp.einsum(
        "rxgsu,ruxd->rsxgd", weights_fresh, value_new, preferred_element_type=jnp.float32
    )
    blended = blended / jnp.transpose(denom, (0, 3, 1, 2, 4))
    return blended.astype(jnp.bfloat16).reshape(
        batch_rows, steps, kv_heads * sharing_factor * HEAD_SIZE
    )


def exchange_kernel(sizes, tok_ref, gain_ref, w_ref, o_ref, sent, held, squares, squares_in, pair_out, pair_in, total,
                    line_out, line_in, sq_s, sq_r, tok_s, tok_r, fx_s, fc_s, pair_s, pair_r, line_s, line_r):
    grp, tp, fs = sizes
    line = grp // 2
    g, t, f = lax.axis_index("grp"), lax.axis_index("tp"), lax.axis_index("fs")
    z, y = g // 2, lax.rem(g, 2)
    rows, width = tok_ref.shape
    depth = w_ref.shape[0]
    blocks = width // depth
    piece = rows // PIECES
    me = t * fs + f
    owner = g // blocks
    owner_t, owner_f = owner // fs, lax.rem(owner, fs)

    def remote(src, dst, ss, rs, device):
        return pltpu.make_async_remote_copy(
            src_ref=src, dst_ref=dst, send_sem=ss, recv_sem=rs, device_id=device, device_id_type=MESH_ID
        )

    barrier = pltpu.get_barrier_semaphore()
    peers = [(lax.rem(g + i, grp), t, f) for i in range(1, grp)]
    mates = [(g, 1 - t, f), (g, t, 1 - f), (g, 1 - t, 1 - f)]
    for device in peers + mates:
        pl.semaphore_signal(barrier, inc=1, device_id=device, device_id_type=MESH_ID)

    wide = tok_ref[...].astype(jnp.float32)
    wide = wide * wide
    part = wide[:, :128]
    for i in range(1, width // 128):
        part = part + wide[:, i * 128 : (i + 1) * 128]
    squares[...] = jnp.broadcast_to(jnp.sum(part.T, axis=0, keepdims=True), squares.shape)
    pl.semaphore_wait(barrier, len(peers) + len(mates))
    sq = [remote(squares, squares_in.at[i], sq_s.at[i], sq_r.at[i], mates[i]) for i in range(3)]
    for copy in sq:
        copy.start()
    for copy in sq:
        copy.wait()
    summed = (squares[...] + squares_in[0]) + (squares_in[1] + squares_in[2])
    scale = lax.rsqrt(summed / (width * tp * fs) + norm_eps)
    scale = jnp.broadcast_to(scale[0:1], (128, rows)).T[:, :1]

    for c in range(PIECES):
        window = pl.ds(c * piece, piece)
        for j in range(blocks):
            cols = pl.ds(j * depth, depth)
            sent[j, window, :] = (
                tok_ref[window, cols].astype(jnp.float32)
                * scale[c * piece : (c + 1) * piece]
                * gain_ref[:, cols].astype(jnp.float32)
            ).astype(jnp.bfloat16)
        for j in range(blocks):
            dest = me * blocks + j

            @pl.when(dest != g)
            def _(c=c, j=j, dest=dest, window=window):
                remote(sent.at[j, window], held.at[g, window], tok_s.at[j, c], tok_r.at[g, c], (dest, t, f)).start()

            @pl.when(dest == g)
            def _(c=c, j=j, window=window):
                pltpu.make_async_copy(sent.at[j, window], held.at[g, window], tok_r.at[g, c]).start()

    def order(i):
        return [0, *[d for k in range(1, line) for d in ((k, line - k) if k < line - k else (k,)) if k <= line - k]][i]

    def forward(slot, window, k, c, end):
        across = remote(held.at[slot, window], held.at[slot, window], fx_s.at[k, c], tok_r.at[slot, c], mates[1])
        beside = remote(held.at[slot, window], held.at[slot, window], fc_s.at[k, c], tok_r.at[slot, c], mates[0])

        @pl.when((t == owner_t) & (f == owner_f))
        def _():
            across.wait_send() if end else across.start()

        @pl.when(t == owner_t)
        def _():
            beside.wait_send() if end else beside.start()

    def pair_copy(i):
        return remote(pair_out.at[i], pair_in.at[i], pair_s.at[i], pair_r.at[i], (z * 2 + 1 - y, t, f))

    def line_copy(i):
        return remote(
            line_out.at[i], line_in.at[i], line_s.at[i], line_r.at[i], (lax.rem(z + order(i), line) * 2 + y, t, f)
        )

    def combine(i):
        pair_copy(i).wait_recv()
        both = total[i] + pair_in[i].astype(jnp.float32)
        if i == 0:
            total[0] = both
        else:
            line_out[i] = both.astype(jnp.bfloat16)
            line_copy(i).start()

    for i in range(line):
        zs = lax.rem(z + order(i), line)
        for k, slot in enumerate((zs * 2 + 1 - y, zs * 2 + y)):
            for c in range(PIECES):
                window = pl.ds(c * piece, piece)
                remote(
                    held.at[slot, window], held.at[slot, window], fx_s.at[0, 0], tok_r.at[slot, c], mates[1]
                ).wait_recv()
                forward(slot, window, 2 * i + k, c, False)
            product = jnp.dot(held[slot], w_ref[...], preferred_element_type=jnp.float32)
            if k == 0:
                pair_out[i] = product.astype(jnp.bfloat16)
                pair_copy(i).start()
            else:
                total[i] = product
        if i > 0:
            combine(i - 1)
    combine(line - 1)
    result = total[0]
    for i in range(1, line):
        line_copy(i).wait_recv()
        result = result + line_in[i].astype(jnp.float32)
    o_ref[...] = result

    for c in range(PIECES):
        window = pl.ds(c * piece, piece)
        for j in range(blocks):
            dest = me * blocks + j

            @pl.when(dest != g)
            def _(c=c, j=j, dest=dest, window=window):
                remote(
                    sent.at[j, window], held.at[g, window], tok_s.at[j, c], tok_r.at[g, c], (dest, t, f)
                ).wait_send()

    for i in range(line):
        zs = lax.rem(z + order(i), line)
        for k, slot in enumerate((zs * 2 + 1 - y, zs * 2 + y)):
            for c in range(PIECES):
                forward(slot, pl.ds(c * piece, piece), 2 * i + k, c, True)
        pair_copy(i).wait_send()
        if i > 0:
            line_copy(i).wait_send()


def exchange(sizes, tokens, gain, layer):
    grp, _, _ = sizes
    rows, width = tokens.shape
    depth, columns = layer.shape
    blocks, line = width // depth, grp // 2
    dma = pltpu.SemaphoreType.DMA
    vmem = pl.BlockSpec(memory_space=pltpu.VMEM)
    return pl.pallas_call(
        functools.partial(exchange_kernel, sizes),
        out_shape=jax.ShapeDtypeStruct((rows, columns), jnp.float32),
        in_specs=[vmem] * 3,
        out_specs=vmem,
        scratch_shapes=[
            pltpu.VMEM((blocks, rows, depth), jnp.bfloat16),
            pltpu.VMEM((grp, rows, depth), jnp.bfloat16),
            pltpu.VMEM((8, rows), jnp.float32),
            pltpu.VMEM((3, 8, rows), jnp.float32),
            pltpu.VMEM((line, rows, columns), jnp.bfloat16),
            pltpu.VMEM((line, rows, columns), jnp.bfloat16),
            pltpu.VMEM((line, rows, columns), jnp.float32),
            pltpu.VMEM((line, rows, columns), jnp.bfloat16),
            pltpu.VMEM((line, rows, columns), jnp.bfloat16),
            dma((3,)),
            dma((3,)),
            dma((blocks, PIECES)),
            dma((grp, PIECES)),
            dma((grp, PIECES)),
            dma((grp, PIECES)),
            dma((line,)),
            dma((line,)),
            dma((line,)),
            dma((line,)),
        ],
        compiler_params=pltpu.CompilerParams(collective_id=0, has_side_effects=True, vmem_limit_bytes=48 << 20),
    )(tokens, gain, layer)


def project(sizes, tokens, norm_gain, layer_half):
    batch_rows, steps, width = tokens.shape
    return exchange(sizes, tokens.reshape(batch_rows * steps, width), norm_gain.reshape(1, width), layer_half)


def fits(sizes, tokens, layer_half):
    grp, tp, fs = sizes
    rows, width, depth = tokens.shape[0] * tokens.shape[1], tokens.shape[2], layer_half.shape[0]
    return (
        tp == 2 and fs == 2 and grp % 2 == 0 and 4 <= grp <= 16 and depth % 128 == 0 and width % depth == 0
        and rows % (128 * PIECES) == 0 and layer_half.shape[1] % 128 == 0
    )


def project_gathered(tokens, norm_gain, layer_half):
    batch_rows, steps = (tokens.shape[0], tokens.shape[1])
    widened, gain_whole = (
        lax.all_gather(tokens, ("tp", "fs"), axis=2, tiled=True),
        lax.all_gather(norm_gain, ("tp", "fs"), axis=0, tiled=True),
    )
    mean_square = (
        jnp.einsum("rsd,rsd->rs", widened, widened, preferred_element_type=jnp.float32)[..., None]
        / MODEL_WIDTH
    )
    normed = (widened * lax.rsqrt(mean_square + norm_eps) * gain_whole.astype(jnp.float32)).astype(
        jnp.bfloat16
    )
    flattened = normed.reshape(batch_rows * steps, MODEL_WIDTH)
    gathered = lax.all_gather(layer_half, "grp", axis=0, tiled=True)
    return jnp.dot(flattened, gathered, preferred_element_type=jnp.float32)


def shards(
    sizes,
    tokens,
    norm_gain,
    queries,
    rotated_key_cache,
    head_value_cache,
    lengths,
    master,
    moment_first,
    moment_second,
    gradient,
):
    average = beta_first * moment_first + (1.0 - beta_first) * gradient
    variance = beta_second * moment_second + (1.0 - beta_second) * gradient * gradient
    update = average / correct_first / (jnp.sqrt(variance / correct_second) + adam_eps)
    renewed = master - learn_rate * (update + decay_rate * master)
    layer_half = renewed.astype(jnp.bfloat16)
    batch_rows, steps = (tokens.shape[0], tokens.shape[1])
    columns = layer_half.shape[1]
    if fits(sizes, tokens, layer_half):
        projected_output = project(sizes, tokens, norm_gain, layer_half)
    else:
        projected_output = project_gathered(tokens, norm_gain, layer_half)
    kv_heads = columns // (2 * HEAD_SIZE)
    projected_output = projected_output.reshape(batch_rows, steps, kv_heads, 2, HEAD_SIZE)
    positions = (lengths[:, None] + jnp.arange(steps, dtype=jnp.int32)[None, :]).astype(jnp.float32)
    key_new = rotate(projected_output[:, :, :, 0, :], positions).astype(jnp.bfloat16)
    value_new = projected_output[:, :, :, 1, :].astype(jnp.bfloat16)
    appended = jnp.stack([key_new, value_new], axis=3).reshape(batch_rows, steps, columns)
    attended = attention(queries, rotated_key_cache, head_value_cache, key_new, value_new, lengths)
    return (attended, appended, renewed, average, variance)


def solution(mesh):
    in_specs = (
        P("grp", None, ("tp", "fs")),
        P(("tp", "fs")),
        P("grp", None, ("tp", "fs")),
        P("grp", None, ("tp", "fs")),
        P("grp", None, ("tp", "fs")),
        P("grp"),
        P("grp", ("tp", "fs")),
        P("grp", ("tp", "fs")),
        P("grp", ("tp", "fs")),
        P("grp", ("tp", "fs")),
    )
    out_specs = (
        P("grp", None, ("tp", "fs")),
        P("grp", None, ("tp", "fs")),
        P("grp", ("tp", "fs")),
        P("grp", ("tp", "fs")),
        P("grp", ("tp", "fs")),
    )
    return jax.shard_map(
        functools.partial(shards, tuple(mesh.shape[name] for name in ("grp", "tp", "fs"))), mesh=mesh, in_specs=in_specs, out_specs=out_specs, check_vma=False,
    )
```

```python
import functools

import jax
import jax.numpy as jnp
from jax import lax
from jax.experimental import pallas as pl
from jax.experimental.pallas import tpu as pltpu
from jax.sharding import PartitionSpec as P

MESH_ID = pl.DeviceIdType.MESH
PIECES = 4

MODEL_WIDTH = 8192
QUERY_HEADS = 64
KEY_VALUE_HEADS = 8
HEAD_SIZE = 128


beta_first = 0.9
beta_second = 0.999
correct_first = 0.9999734386011124
correct_second = 0.09520785288629038
adam_eps = 1e-08
learn_rate = 0.003
decay_rate = 0.1
norm_eps = 1e-06
rope_base = 1000000.0


def rotate(keys, positions):
    halfway = keys.shape[-1] // 2
    frequency = rope_base ** (-(jnp.arange(halfway, dtype=jnp.float32) * 2.0 / keys.shape[-1]))
    angles = positions[:, :, None] * frequency[None, None, :]
    cosine = jnp.cos(angles)[:, :, None, :]
    sine = jnp.sin(angles)[:, :, None, :]
    first_half = keys[..., :halfway]
    second_half = keys[..., halfway:]
    return jnp.concatenate(
        [first_half * cosine - second_half * sine, second_half * cosine + first_half * sine],
        axis=-1,
    )


def attention(queries, rotated_key_cache, head_value_cache, key_new, value_new, lengths):
    batch_rows, steps = (queries.shape[0], queries.shape[1])
    window = rotated_key_cache.shape[1]
    kv_heads = rotated_key_cache.shape[2] // HEAD_SIZE
    sharing_factor = QUERY_HEADS // KEY_VALUE_HEADS
    factor = HEAD_SIZE ** (-0.5)
    query_heads = queries.reshape(batch_rows, steps, kv_heads, sharing_factor, HEAD_SIZE)
    cache_key_seeds = rotated_key_cache.reshape(batch_rows, window, kv_heads, HEAD_SIZE)
    cache_values = head_value_cache.reshape(batch_rows, window, kv_heads, HEAD_SIZE)
    scores_cached = (
        jnp.einsum(
            "rsxgd,rlxd->rxgsl", query_heads, cache_key_seeds, preferred_element_type=jnp.float32
        )
        * factor
    )
    scores_fresh = (
        jnp.einsum("rsxgd,ruxd->rxgsu", query_heads, key_new, preferred_element_type=jnp.float32)
        * factor
    )
    present = (jnp.arange(window, dtype=jnp.int32)[None, :] < lengths[:, None])[
        :, None, None, None, :
    ]
    causal = (
        jnp.arange(steps, dtype=jnp.int32)[None, :] <= jnp.arange(steps, dtype=jnp.int32)[:, None]
    )[None, None, None, :, :]
    scores_cached = jnp.where(present, scores_cached, -jnp.inf)
    scores_fresh = jnp.where(causal, scores_fresh, -jnp.inf)
    ceiling = jnp.maximum(
        jnp.max(scores_cached, axis=-1, keepdims=True),
        jnp.max(scores_fresh, axis=-1, keepdims=True),
    )
    probs_cached = jnp.exp(scores_cached - ceiling)
    probs_fresh = jnp.exp(scores_fresh - ceiling)
    denom = jnp.sum(probs_cached, axis=-1, keepdims=True) + jnp.sum(
        probs_fresh, axis=-1, keepdims=True
    )
    weights_cached = probs_cached.astype(jnp.bfloat16)
    weights_fresh = probs_fresh.astype(jnp.bfloat16)
    blended = jnp.einsum(
        "rxgsl,rlxd->rsxgd", weights_cached, cache_values, preferred_element_type=jnp.float32
    )
    blended = blended + jnp.einsum(
        "rxgsu,ruxd->rsxgd", weights_fresh, value_new, preferred_element_type=jnp.float32
    )
    blended = blended / jnp.transpose(denom, (0, 3, 1, 2, 4))
    return blended.astype(jnp.bfloat16).reshape(
        batch_rows, steps, kv_heads * sharing_factor * HEAD_SIZE
    )


def exchange_kernel(sizes, tok_ref, gain_ref, w_ref, cos_ref, sin_ref, present_ref, q_hbm, k_hbm, v_hbm, out_ref, app_ref,
                    sent, held, squares, squares_in, pair_out, pair_in, total, line_out, line_in, q_ref, k_ref, v_ref,
                    part_out, part_max, part_sum, sq_s, sq_r, tok_s, tok_r, fx_s, fc_s, side_s, pair_s, pair_r, line_s, line_r,
                    load_s):
    grp, tp, fs = sizes
    line = grp // 2
    g, t, f = lax.axis_index("grp"), lax.axis_index("tp"), lax.axis_index("fs")
    z, y = g // 2, lax.rem(g, 2)
    rows, width = tok_ref.shape
    depth = w_ref.shape[0]
    blocks = width // depth
    piece = rows // PIECES
    me = t * fs + f
    owner = g // blocks
    owner_t, owner_f = owner // fs, lax.rem(owner, fs)

    def remote(src, dst, ss, rs, device):
        return pltpu.make_async_remote_copy(
            src_ref=src, dst_ref=dst, send_sem=ss, recv_sem=rs, device_id=device, device_id_type=MESH_ID
        )

    barrier = pltpu.get_barrier_semaphore()
    peers = [(lax.rem(g + i, grp), t, f) for i in range(1, grp)]
    mates = [(g, 1 - t, f), (g, t, 1 - f), (g, 1 - t, 1 - f)]
    beside_z = z + 1 - 2 * lax.rem(z, 2)
    sides = [(beside_z * 2 + i, t, 1 - f) for i in range(2)]
    loads = [
        pltpu.make_async_copy(src, dst, load_s.at[i])
        for i, (src, dst) in enumerate(((q_hbm, q_ref), (k_hbm, k_ref), (v_hbm, v_ref)))
    ]
    for copy in loads:
        copy.start()
    for device in peers + mates + sides:
        pl.semaphore_signal(barrier, inc=1, device_id=device, device_id_type=MESH_ID)

    wide = tok_ref[...].astype(jnp.float32)
    wide = wide * wide
    part = wide[:, :128]
    for i in range(1, width // 128):
        part = part + wide[:, i * 128 : (i + 1) * 128]
    squares[...] = jnp.broadcast_to(jnp.sum(part.T, axis=0, keepdims=True), squares.shape)
    pl.semaphore_wait(barrier, len(peers) + len(mates) + len(sides))
    sq = [remote(squares, squares_in.at[i], sq_s.at[i], sq_r.at[i], mates[i]) for i in range(3)]
    for copy in sq:
        copy.start()
    for copy in sq:
        copy.wait()
    summed = (squares[...] + squares_in[0]) + (squares_in[1] + squares_in[2])
    scale = lax.rsqrt(summed / (width * tp * fs) + norm_eps)
    scale = jnp.broadcast_to(scale[0:1], (128, rows)).T[:, :1]

    def send_block(c, j, end):
        dest = me * blocks + j
        window = pl.ds(c * piece, piece)
        src, dst = sent.at[j, window], held.at[g, window]
        away = remote(src, dst, tok_s.at[j, c], tok_r.at[g, c], (dest, t, f))
        side = remote(src, dst, side_s.at[j, c], tok_r.at[g, c], (dest, t, 1 - f))

        @pl.when(dest != g)
        def _():
            away.wait_send() if end else away.start()

        @pl.when(dest // 2 == beside_z)
        def _():
            side.wait_send() if end else side.start()

        if not end:

            @pl.when(dest == g)
            def _():
                pltpu.make_async_copy(src, dst, tok_r.at[g, c]).start()

    for c in range(PIECES):
        window = pl.ds(c * piece, piece)
        for j in range(blocks):
            cols = pl.ds(j * depth, depth)
            sent[j, window, :] = (
                tok_ref[window, cols].astype(jnp.float32)
                * scale[c * piece : (c + 1) * piece]
                * gain_ref[:, cols].astype(jnp.float32)
            ).astype(jnp.bfloat16)
        for j in range(blocks):
            send_block(c, j, False)

    def order(i):
        return [0, *[d for k in range(1, line) for d in ((k, line - k) if k < line - k else (k,)) if k <= line - k]][i]

    def forward(slot, window, k, c, end):
        across = remote(held.at[slot, window], held.at[slot, window], fx_s.at[k, c], tok_r.at[slot, c], mates[1])
        beside = remote(held.at[slot, window], held.at[slot, window], fc_s.at[k, c], tok_r.at[slot, c], mates[0])

        @pl.when((t == owner_t) & (f == owner_f) & (slot // 2 != beside_z))
        def _():
            across.wait_send() if end else across.start()

        @pl.when(t == owner_t)
        def _():
            beside.wait_send() if end else beside.start()

    def pair_copy(i, c):
        window = pl.ds(c * piece, piece)
        return remote(
            pair_out.at[i, window], pair_in.at[i, window], pair_s.at[i, c], pair_r.at[i, c], (z * 2 + 1 - y, t, f)
        )

    def line_copy(i, c):
        window = pl.ds(c * piece, piece)
        device = (lax.rem(z + order(i), line) * 2 + y, t, f)
        return remote(line_out.at[i, window], line_in.at[i, window], line_s.at[i, c], line_r.at[i, c], device)

    def combine(i, c):
        window = pl.ds(c * piece, piece)
        pair_copy(i, c).wait_recv()
        both = total[i, window] + pair_in[i, window].astype(jnp.float32)
        if i == 0:
            total[0, window] = both
        else:
            line_out[i, window] = both.astype(jnp.bfloat16)
            line_copy(i, c).start()

    batch_rows, slots, kv_width = k_ref.shape
    steps = rows // batch_rows
    kv_heads = kv_width // HEAD_SIZE
    share = q_ref.shape[1] // kv_width
    few = 128 // slots
    band = few * steps
    factor = HEAD_SIZE ** (-0.5)
    chunks = batch_rows // few
    over_last = (((1,), (1,)), ((), ()))

    def head_lanes(x, h):
        return pl.ds((x * share + h) * HEAD_SIZE, HEAD_SIZE)

    def some_queries(b, x):
        return jnp.concatenate([q_ref[pl.ds(b * band, band), head_lanes(x, h)] for h in range(share)], axis=0)

    def attend_cached(b):
        shape = (share * band, few * slots)
        row = lax.rem(lax.broadcasted_iota(jnp.int32, shape, 0), band) // steps
        same = row == lax.broadcasted_iota(jnp.int32, shape, 1) // slots
        valid = same & (present_ref[pl.ds(b, 1), :] > 0.5)
        for x in range(kv_heads):
            lanes = pl.ds(x * HEAD_SIZE, HEAD_SIZE)
            keys = k_ref[pl.ds(b * few, few), :, lanes].reshape(few * slots, HEAD_SIZE)
            values = v_ref[pl.ds(b * few, few), :, lanes].reshape(few * slots, HEAD_SIZE)
            scores = (
                lax.dot_general(some_queries(b, x), keys, over_last, preferred_element_type=jnp.float32) * factor
            )
            scores = jnp.where(valid, scores, -jnp.inf)
            most = jnp.max(scores, axis=1, keepdims=True)
            probs = jnp.exp(scores - most)
            part_max[b, x] = jnp.broadcast_to(most, (share * band, HEAD_SIZE))
            part_sum[b, x] = jnp.broadcast_to(jnp.sum(probs, axis=1, keepdims=True), (share * band, HEAD_SIZE))
            part_out[b, x] = jnp.dot(probs.astype(jnp.bfloat16), values, preferred_element_type=jnp.float32)

    def attend_new(b):
        shape = (share * band, band)
        mine = lax.rem(lax.broadcasted_iota(jnp.int32, shape, 0), band)
        other = lax.broadcasted_iota(jnp.int32, shape, 1)
        valid = (mine // steps == other // steps) & (other <= mine)
        window = pl.ds(b * band, band)
        for x in range(kv_heads):
            keys = app_ref[window, pl.ds(2 * x * HEAD_SIZE, HEAD_SIZE)]
            values = app_ref[window, pl.ds((2 * x + 1) * HEAD_SIZE, HEAD_SIZE)]
            scores = (
                lax.dot_general(some_queries(b, x), keys, over_last, preferred_element_type=jnp.float32) * factor
            )
            scores = jnp.where(valid, scores, -jnp.inf)
            before = part_max[b, x]
            most = jnp.maximum(before, jnp.max(scores, axis=1, keepdims=True))
            probs = jnp.exp(scores - most[:, :1])
            again = jnp.exp(before - most)
            denom = again * part_sum[b, x] + jnp.sum(probs, axis=1, keepdims=True)
            blended = again * part_out[b, x] + jnp.dot(
                probs.astype(jnp.bfloat16), values, preferred_element_type=jnp.float32
            )
            blended = (blended / denom).astype(jnp.bfloat16)
            for h in range(share):
                out_ref[window, head_lanes(x, h)] = blended[h * band : (h + 1) * band]

    late = None
    done = 0
    for c in range(PIECES):
        window = pl.ds(c * piece, piece)
        for i in range(line):
            zs = lax.rem(z + order(i), line)
            for k, slot in enumerate((zs * 2 + 1 - y, zs * 2 + y)):
                remote(
                    held.at[slot, window], held.at[slot, window], fx_s.at[0, 0], tok_r.at[slot, c], mates[1]
                ).wait_recv()
                forward(slot, window, 2 * i + k, c, False)
                product = jnp.dot(held[slot, window], w_ref[...], preferred_element_type=jnp.float32)
                if k == 0:
                    pair_out[i, window] = product.astype(jnp.bfloat16)
                    pair_copy(i, c).start()
                else:
                    total[i, window] = product
            if late is not None:
                combine(*late)
            late = (i, c)
            if c == 0 and i == 0:
                for copy in loads:
                    copy.wait()
            steps_now = -(-chunks // (line * PIECES))
            for b in range(done, min(done + steps_now, chunks)):
                attend_cached(b)
            done = min(done + steps_now, chunks)
    combine(*late)

    half = HEAD_SIZE // 2
    for c in range(PIECES):
        window = pl.ds(c * piece, piece)
        result = total[0, window]
        for i in range(1, line):
            line_copy(i, c).wait_recv()
            result = result + line_in[i, window].astype(jnp.float32)
        for x in range(kv_heads):
            key = result[:, 2 * x * HEAD_SIZE : (2 * x + 1) * HEAD_SIZE]
            key = key * cos_ref[window, :] + pltpu.roll(key, half, 1) * sin_ref[window, :]
            app_ref[window, pl.ds(2 * x * HEAD_SIZE, HEAD_SIZE)] = key.astype(jnp.bfloat16)
            app_ref[window, pl.ds((2 * x + 1) * HEAD_SIZE, HEAD_SIZE)] = result[
                :, (2 * x + 1) * HEAD_SIZE : (2 * x + 2) * HEAD_SIZE
            ].astype(jnp.bfloat16)
        for b in range(c * chunks // PIECES, (c + 1) * chunks // PIECES):
            attend_new(b)

    for c in range(PIECES):
        for j in range(blocks):
            send_block(c, j, True)
        for i in range(line):
            zs = lax.rem(z + order(i), line)
            for k, slot in enumerate((zs * 2 + 1 - y, zs * 2 + y)):
                forward(slot, pl.ds(c * piece, piece), 2 * i + k, c, True)
            pair_copy(i, c).wait_send()
            if i > 0:
                line_copy(i, c).wait_send()


def project_and_attend(sizes, tokens, norm_gain, layer, queries, key_cache, value_cache, lengths):
    grp, _, _ = sizes
    batch_rows, steps, width = tokens.shape
    _, slots, kv_width = key_cache.shape
    rows = batch_rows * steps
    depth, columns = layer.shape
    blocks, line = width // depth, grp // 2
    kv_heads, share = kv_width // HEAD_SIZE, queries.shape[2] // kv_width
    few = 128 // slots
    half = HEAD_SIZE // 2
    positions = (lengths[:, None] + jnp.arange(steps, dtype=jnp.int32)[None, :]).astype(jnp.float32)
    frequency = rope_base ** (-(jnp.arange(half, dtype=jnp.float32) * 2.0 / HEAD_SIZE))
    angles = positions.reshape(rows, 1) * frequency[None, :]
    cosine, sine = jnp.cos(angles), jnp.sin(angles)
    cosine = jnp.concatenate([cosine, cosine], axis=1)
    sine = jnp.concatenate([-sine, sine], axis=1)
    present = (jnp.arange(slots, dtype=jnp.int32)[None, :] < lengths[:, None]).astype(jnp.float32)
    present = present.reshape(batch_rows // few, few * slots)
    dma = pltpu.SemaphoreType.DMA
    vmem = pl.BlockSpec(memory_space=pltpu.VMEM)
    anywhere = pl.BlockSpec(memory_space=pl.ANY)
    flat_queries = queries.reshape(rows, queries.shape[2])
    part = pltpu.VMEM((batch_rows // few, kv_heads, share * few * steps, HEAD_SIZE), jnp.float32)
    attended, appended = pl.pallas_call(
        functools.partial(exchange_kernel, sizes),
        out_shape=(
            jax.ShapeDtypeStruct(flat_queries.shape, jnp.bfloat16),
            jax.ShapeDtypeStruct((rows, columns), jnp.bfloat16),
        ),
        in_specs=[vmem] * 6 + [anywhere] * 3,
        out_specs=(vmem, vmem),
        scratch_shapes=[
            pltpu.VMEM((blocks, rows, depth), jnp.bfloat16),
            pltpu.VMEM((grp, rows, depth), jnp.bfloat16),
            pltpu.VMEM((8, rows), jnp.float32),
            pltpu.VMEM((3, 8, rows), jnp.float32),
            pltpu.VMEM((line, rows, columns), jnp.bfloat16),
            pltpu.VMEM((line, rows, columns), jnp.bfloat16),
            pltpu.VMEM((line, rows, columns), jnp.float32),
            pltpu.VMEM((line, rows, columns), jnp.bfloat16),
            pltpu.VMEM((line, rows, columns), jnp.bfloat16),
            pltpu.VMEM(flat_queries.shape, jnp.bfloat16),
            pltpu.VMEM(key_cache.shape, jnp.bfloat16),
            pltpu.VMEM(value_cache.shape, jnp.bfloat16),
            part,
            part,
            part,
            dma((3,)),
            dma((3,)),
            dma((blocks, PIECES)),
            dma((grp, PIECES)),
            dma((grp, PIECES)),
            dma((grp, PIECES)),
            dma((blocks, PIECES)),
            dma((line, PIECES)),
            dma((line, PIECES)),
            dma((line, PIECES)),
            dma((line, PIECES)),
            dma((3,)),
        ],
        compiler_params=pltpu.CompilerParams(collective_id=0, has_side_effects=True, vmem_limit_bytes=48 << 20),
    )(
        tokens.reshape(rows, width), norm_gain.reshape(1, width), layer, cosine, sine, present, flat_queries, key_cache,
        value_cache,
    )
    return attended.reshape(queries.shape), appended.reshape(batch_rows, steps, columns)


def fits(sizes, tokens, layer_half, queries, key_cache):
    grp, tp, fs = sizes
    batch_rows, steps, width = tokens.shape
    rows, depth, columns = batch_rows * steps, layer_half.shape[0], layer_half.shape[1]
    slots, kv_width = key_cache.shape[1:]
    if tp != 2 or fs != 2 or grp % 4 or not 4 <= grp <= 16 or 128 % slots or slots % 16:
        return False
    few = 128 // slots
    return (
        depth % 128 == 0 and width % depth == 0 and rows % 128 == 0 and rows % (16 * PIECES) == 0
        and columns == 2 * kv_width and few * steps % 16 == 0 and batch_rows % (few * PIECES) == 0
        and queries.shape[2] % kv_width == 0
    )


def project_gathered(tokens, norm_gain, layer_half):
    batch_rows, steps = (tokens.shape[0], tokens.shape[1])
    widened, gain_whole = (
        lax.all_gather(tokens, ("tp", "fs"), axis=2, tiled=True),
        lax.all_gather(norm_gain, ("tp", "fs"), axis=0, tiled=True),
    )
    mean_square = (
        jnp.einsum("rsd,rsd->rs", widened, widened, preferred_element_type=jnp.float32)[..., None]
        / MODEL_WIDTH
    )
    normed = (widened * lax.rsqrt(mean_square + norm_eps) * gain_whole.astype(jnp.float32)).astype(
        jnp.bfloat16
    )
    flattened = normed.reshape(batch_rows * steps, MODEL_WIDTH)
    gathered = lax.all_gather(layer_half, "grp", axis=0, tiled=True)
    return jnp.dot(flattened, gathered, preferred_element_type=jnp.float32)


def shards(
    sizes,
    tokens,
    norm_gain,
    queries,
    rotated_key_cache,
    head_value_cache,
    lengths,
    master,
    moment_first,
    moment_second,
    gradient,
):
    average = beta_first * moment_first + (1.0 - beta_first) * gradient
    variance = beta_second * moment_second + (1.0 - beta_second) * gradient * gradient
    update = average / correct_first / (jnp.sqrt(variance / correct_second) + adam_eps)
    renewed = master - learn_rate * (update + decay_rate * master)
    layer_half = renewed.astype(jnp.bfloat16)
    batch_rows, steps = (tokens.shape[0], tokens.shape[1])
    columns = layer_half.shape[1]
    if fits(sizes, tokens, layer_half, queries, rotated_key_cache):
        attended, appended = project_and_attend(
            sizes, tokens, norm_gain, layer_half, queries, rotated_key_cache, head_value_cache, lengths
        )
        return (attended, appended, renewed, average, variance)
    projected_output = project_gathered(tokens, norm_gain, layer_half)
    kv_heads = columns // (2 * HEAD_SIZE)
    projected_output = projected_output.reshape(batch_rows, steps, kv_heads, 2, HEAD_SIZE)
    positions = (lengths[:, None] + jnp.arange(steps, dtype=jnp.int32)[None, :]).astype(jnp.float32)
    key_new = rotate(projected_output[:, :, :, 0, :], positions).astype(jnp.bfloat16)
    value_new = projected_output[:, :, :, 1, :].astype(jnp.bfloat16)
    appended = jnp.stack([key_new, value_new], axis=3).reshape(batch_rows, steps, columns)
    attended = attention(queries, rotated_key_cache, head_value_cache, key_new, value_new, lengths)
    return (attended, appended, renewed, average, variance)


def solution(mesh):
    in_specs = (
        P("grp", None, ("tp", "fs")),
        P(("tp", "fs")),
        P("grp", None, ("tp", "fs")),
        P("grp", None, ("tp", "fs")),
        P("grp", None, ("tp", "fs")),
        P("grp"),
        P("grp", ("tp", "fs")),
        P("grp", ("tp", "fs")),
        P("grp", ("tp", "fs")),
        P("grp", ("tp", "fs")),
    )
    out_specs = (
        P("grp", None, ("tp", "fs")),
        P("grp", None, ("tp", "fs")),
        P("grp", ("tp", "fs")),
        P("grp", ("tp", "fs")),
        P("grp", ("tp", "fs")),
    )
    return jax.shard_map(
        functools.partial(shards, tuple(mesh.shape[name] for name in ("grp", "tp", "fs"))), mesh=mesh, in_specs=in_specs, out_specs=out_specs, check_vma=False,
    )
```

```python
import functools

import jax
import jax.numpy as jnp
from jax import lax
from jax.experimental import pallas as pl
from jax.experimental.pallas import tpu as pltpu
from jax.sharding import PartitionSpec as P

MESH_ID = pl.DeviceIdType.MESH
PIECES = 4

MODEL_WIDTH = 8192
QUERY_HEADS = 64
KEY_VALUE_HEADS = 8
HEAD_SIZE = 128


beta_first = 0.9
beta_second = 0.999
correct_first = 0.9999734386011124
correct_second = 0.09520785288629038
adam_eps = 1e-08
learn_rate = 0.003
decay_rate = 0.1
norm_eps = 1e-06
rope_base = 1000000.0


def rotate(keys, positions):
    halfway = keys.shape[-1] // 2
    frequency = rope_base ** (-(jnp.arange(halfway, dtype=jnp.float32) * 2.0 / keys.shape[-1]))
    angles = positions[:, :, None] * frequency[None, None, :]
    cosine = jnp.cos(angles)[:, :, None, :]
    sine = jnp.sin(angles)[:, :, None, :]
    first_half = keys[..., :halfway]
    second_half = keys[..., halfway:]
    return jnp.concatenate(
        [first_half * cosine - second_half * sine, second_half * cosine + first_half * sine],
        axis=-1,
    )


def attention(queries, rotated_key_cache, head_value_cache, key_new, value_new, lengths):
    batch_rows, steps = (queries.shape[0], queries.shape[1])
    window = rotated_key_cache.shape[1]
    kv_heads = rotated_key_cache.shape[2] // HEAD_SIZE
    sharing_factor = QUERY_HEADS // KEY_VALUE_HEADS
    factor = HEAD_SIZE ** (-0.5)
    query_heads = queries.reshape(batch_rows, steps, kv_heads, sharing_factor, HEAD_SIZE)
    cache_key_seeds = rotated_key_cache.reshape(batch_rows, window, kv_heads, HEAD_SIZE)
    cache_values = head_value_cache.reshape(batch_rows, window, kv_heads, HEAD_SIZE)
    scores_cached = (
        jnp.einsum(
            "rsxgd,rlxd->rxgsl", query_heads, cache_key_seeds, preferred_element_type=jnp.float32
        )
        * factor
    )
    scores_fresh = (
        jnp.einsum("rsxgd,ruxd->rxgsu", query_heads, key_new, preferred_element_type=jnp.float32)
        * factor
    )
    present = (jnp.arange(window, dtype=jnp.int32)[None, :] < lengths[:, None])[
        :, None, None, None, :
    ]
    causal = (
        jnp.arange(steps, dtype=jnp.int32)[None, :] <= jnp.arange(steps, dtype=jnp.int32)[:, None]
    )[None, None, None, :, :]
    scores_cached = jnp.where(present, scores_cached, -jnp.inf)
    scores_fresh = jnp.where(causal, scores_fresh, -jnp.inf)
    ceiling = jnp.maximum(
        jnp.max(scores_cached, axis=-1, keepdims=True),
        jnp.max(scores_fresh, axis=-1, keepdims=True),
    )
    probs_cached = jnp.exp(scores_cached - ceiling)
    probs_fresh = jnp.exp(scores_fresh - ceiling)
    denom = jnp.sum(probs_cached, axis=-1, keepdims=True) + jnp.sum(
        probs_fresh, axis=-1, keepdims=True
    )
    weights_cached = probs_cached.astype(jnp.bfloat16)
    weights_fresh = probs_fresh.astype(jnp.bfloat16)
    blended = jnp.einsum(
        "rxgsl,rlxd->rsxgd", weights_cached, cache_values, preferred_element_type=jnp.float32
    )
    blended = blended + jnp.einsum(
        "rxgsu,ruxd->rsxgd", weights_fresh, value_new, preferred_element_type=jnp.float32
    )
    blended = blended / jnp.transpose(denom, (0, 3, 1, 2, 4))
    return blended.astype(jnp.bfloat16).reshape(
        batch_rows, steps, kv_heads * sharing_factor * HEAD_SIZE
    )


def exchange_kernel(sizes, tok_ref, gain_ref, w_ref, cos_ref, sin_ref, present_ref, q_hbm, k_hbm, v_hbm, out_ref, app_ref,
                    sent, held, squares, squares_in, pair_out, pair_in, total, line_out, line_in, q_ref, k_ref, v_ref,
                    part_out, part_max, part_sum, sq_s, sq_r, tok_s, tok_r, fx_s, fc_s, pair_s, pair_r, line_s, line_r,
                    load_s):
    grp, tp, fs = sizes
    line = grp // 2
    g, t, f = lax.axis_index("grp"), lax.axis_index("tp"), lax.axis_index("fs")
    z, y = g // 2, lax.rem(g, 2)
    rows, width = tok_ref.shape
    depth = w_ref.shape[0]
    blocks = width // depth
    piece = rows // PIECES
    me = t * fs + f
    owner = g // blocks
    owner_t, owner_f = owner // fs, lax.rem(owner, fs)

    def remote(src, dst, ss, rs, device):
        return pltpu.make_async_remote_copy(
            src_ref=src, dst_ref=dst, send_sem=ss, recv_sem=rs, device_id=device, device_id_type=MESH_ID
        )

    barrier = pltpu.get_barrier_semaphore()
    peers = [(lax.rem(g + i, grp), t, f) for i in range(1, grp)]
    mates = [(g, 1 - t, f), (g, t, 1 - f), (g, 1 - t, 1 - f)]
    loads = [
        pltpu.make_async_copy(src, dst, load_s.at[i])
        for i, (src, dst) in enumerate(((q_hbm, q_ref), (k_hbm, k_ref), (v_hbm, v_ref)))
    ]
    for copy in loads:
        copy.start()
    for device in peers + mates:
        pl.semaphore_signal(barrier, inc=1, device_id=device, device_id_type=MESH_ID)

    wide = tok_ref[...].astype(jnp.float32)
    wide = wide * wide
    part = wide[:, :128]
    for i in range(1, width // 128):
        part = part + wide[:, i * 128 : (i + 1) * 128]
    squares[...] = jnp.broadcast_to(jnp.sum(part.T, axis=0, keepdims=True), squares.shape)
    pl.semaphore_wait(barrier, len(peers) + len(mates))
    sq = [remote(squares, squares_in.at[i], sq_s.at[i], sq_r.at[i], mates[i]) for i in range(3)]
    for copy in sq:
        copy.start()
    for copy in sq:
        copy.wait()
    summed = (squares[...] + squares_in[0]) + (squares_in[1] + squares_in[2])
    scale = lax.rsqrt(summed / (width * tp * fs) + norm_eps)
    scale = jnp.broadcast_to(scale[0:1], (128, rows)).T[:, :1]

    def send_block(c, j, end):
        dest = me * blocks + j
        window = pl.ds(c * piece, piece)
        src, dst = sent.at[j, window], held.at[g, window]
        away = remote(src, dst, tok_s.at[j, c], tok_r.at[g, c], (dest, t, f))

        @pl.when(dest != g)
        def _():
            away.wait_send() if end else away.start()

        if not end:

            @pl.when(dest == g)
            def _():
                pltpu.make_async_copy(src, dst, tok_r.at[g, c]).start()

    for c in range(PIECES):
        window = pl.ds(c * piece, piece)
        for j in range(blocks):
            cols = pl.ds(j * depth, depth)
            sent[j, window, :] = (
                tok_ref[window, cols].astype(jnp.float32)
                * scale[c * piece : (c + 1) * piece]
                * gain_ref[:, cols].astype(jnp.float32)
            ).astype(jnp.bfloat16)
        if c < 1:
            for j in range(blocks):
                send_block(c, j, False)

    def order(i):
        return [0, *[d for k in range(1, line) for d in ((k, line - k) if k < line - k else (k,)) if k <= line - k]][i]

    def forward(slot, window, k, c, end):
        across = remote(held.at[slot, window], held.at[slot, window], fx_s.at[k, c], tok_r.at[slot, c], mates[1])
        beside = remote(held.at[slot, window], held.at[slot, window], fc_s.at[k, c], tok_r.at[slot, c], mates[0])

        lead = owner_t if c % 2 == 0 else 1 - owner_t

        @pl.when((t == lead) & (f == owner_f))
        def _():
            across.wait_send() if end else across.start()

        @pl.when(((f == owner_f) & (t == owner_t)) | ((f != owner_f) & (t == lead)))
        def _():
            beside.wait_send() if end else beside.start()

    def pair_copy(i, c):
        window = pl.ds(c * piece, piece)
        return remote(
            pair_out.at[i, window], pair_in.at[i, window], pair_s.at[i, c], pair_r.at[i, c], (z * 2 + 1 - y, t, f)
        )

    def line_copy(i, c):
        window = pl.ds(c * piece, piece)
        device = (lax.rem(z + order(i), line) * 2 + y, t, f)
        return remote(line_out.at[i, window], line_in.at[i, window], line_s.at[i, c], line_r.at[i, c], device)

    def combine(i, c):
        window = pl.ds(c * piece, piece)
        pair_copy(i, c).wait_recv()
        both = total[i, window] + pair_in[i, window].astype(jnp.float32)
        if i == 0:
            total[0, window] = both
        else:
            line_out[i, window] = both.astype(jnp.bfloat16)
            line_copy(i, c).start()

    batch_rows, slots, kv_width = k_ref.shape
    steps = rows // batch_rows
    kv_heads = kv_width // HEAD_SIZE
    share = q_ref.shape[1] // kv_width
    few = 128 // slots
    band = few * steps
    factor = HEAD_SIZE ** (-0.5)
    chunks = batch_rows // few
    over_last = (((1,), (1,)), ((), ()))

    def head_lanes(x, h):
        return pl.ds((x * share + h) * HEAD_SIZE, HEAD_SIZE)

    def some_queries(b, x):
        return jnp.concatenate([q_ref[pl.ds(b * band, band), head_lanes(x, h)] for h in range(share)], axis=0)

    def attend_cached(b):
        shape = (share * band, few * slots)
        row = lax.rem(lax.broadcasted_iota(jnp.int32, shape, 0), band) // steps
        same = row == lax.broadcasted_iota(jnp.int32, shape, 1) // slots
        valid = same & (present_ref[pl.ds(b, 1), :] > 0.5)
        for x in range(kv_heads):
            lanes = pl.ds(x * HEAD_SIZE, HEAD_SIZE)
            keys = k_ref[pl.ds(b * few, few), :, lanes].reshape(few * slots, HEAD_SIZE)
            values = v_ref[pl.ds(b * few, few), :, lanes].reshape(few * slots, HEAD_SIZE)
            scores = (
                lax.dot_general(some_queries(b, x), keys, over_last, preferred_element_type=jnp.float32) * factor
            )
            scores = jnp.where(valid, scores, -jnp.inf)
            most = jnp.max(scores, axis=1, keepdims=True)
            probs = jnp.exp(scores - most)
            part_max[b, x] = jnp.broadcast_to(most, (share * band, HEAD_SIZE))
            part_sum[b, x] = jnp.broadcast_to(jnp.sum(probs, axis=1, keepdims=True), (share * band, HEAD_SIZE))
            part_out[b, x] = jnp.dot(probs.astype(jnp.bfloat16), values, preferred_element_type=jnp.float32)

    def attend_new(b):
        shape = (share * band, band)
        mine = lax.rem(lax.broadcasted_iota(jnp.int32, shape, 0), band)
        other = lax.broadcasted_iota(jnp.int32, shape, 1)
        valid = (mine // steps == other // steps) & (other <= mine)
        window = pl.ds(b * band, band)
        for x in range(kv_heads):
            keys = app_ref[window, pl.ds(2 * x * HEAD_SIZE, HEAD_SIZE)]
            values = app_ref[window, pl.ds((2 * x + 1) * HEAD_SIZE, HEAD_SIZE)]
            scores = (
                lax.dot_general(some_queries(b, x), keys, over_last, preferred_element_type=jnp.float32) * factor
            )
            scores = jnp.where(valid, scores, -jnp.inf)
            before = part_max[b, x]
            most = jnp.maximum(before, jnp.max(scores, axis=1, keepdims=True))
            probs = jnp.exp(scores - most[:, :1])
            again = jnp.exp(before - most)
            denom = again * part_sum[b, x] + jnp.sum(probs, axis=1, keepdims=True)
            blended = again * part_out[b, x] + jnp.dot(
                probs.astype(jnp.bfloat16), values, preferred_element_type=jnp.float32
            )
            blended = (blended / denom).astype(jnp.bfloat16)
            for h in range(share):
                out_ref[window, head_lanes(x, h)] = blended[h * band : (h + 1) * band]

    late = None
    done = 0
    for c in range(PIECES):
        window = pl.ds(c * piece, piece)
        if c + 1 < PIECES:
            for j in range(blocks):
                send_block(c, j, True)
                send_block(c + 1, j, False)
        for i in range(line):
            zs = lax.rem(z + order(i), line)
            visits = ((0, zs * 2 + 1 - y), (1, zs * 2 + y))
            for k, slot in visits if i else visits[::-1]:
                remote(
                    held.at[slot, window], held.at[slot, window], fx_s.at[0, 0], tok_r.at[slot, c], mates[1]
                ).wait_recv()
                forward(slot, window, 2 * i + k, c, False)
                product = jnp.dot(held[slot, window], w_ref[...], preferred_element_type=jnp.float32)
                if k == 0:
                    pair_out[i, window] = product.astype(jnp.bfloat16)
                    pair_copy(i, c).start()
                else:
                    total[i, window] = product
            if late is not None:
                combine(*late)
            late = (i, c)
            if c == 0 and i == 0:
                for copy in loads:
                    copy.wait()
            steps_now = -(-chunks // (line * PIECES))
            for b in range(done, min(done + steps_now, chunks)):
                attend_cached(b)
            done = min(done + steps_now, chunks)
    combine(*late)

    half = HEAD_SIZE // 2
    for c in range(PIECES):
        window = pl.ds(c * piece, piece)
        result = total[0, window]
        for i in range(1, line):
            line_copy(i, c).wait_recv()
            result = result + line_in[i, window].astype(jnp.float32)
        for x in range(kv_heads):
            key = result[:, 2 * x * HEAD_SIZE : (2 * x + 1) * HEAD_SIZE]
            key = key * cos_ref[window, :] + pltpu.roll(key, half, 1) * sin_ref[window, :]
            app_ref[window, pl.ds(2 * x * HEAD_SIZE, HEAD_SIZE)] = key.astype(jnp.bfloat16)
            app_ref[window, pl.ds((2 * x + 1) * HEAD_SIZE, HEAD_SIZE)] = result[
                :, (2 * x + 1) * HEAD_SIZE : (2 * x + 2) * HEAD_SIZE
            ].astype(jnp.bfloat16)
        for b in range(c * chunks // PIECES, (c + 1) * chunks // PIECES):
            attend_new(b)

    for c in range(PIECES):
        for j in range(blocks):
            if c + 1 >= PIECES:
                send_block(c, j, True)
        for i in range(line):
            zs = lax.rem(z + order(i), line)
            for k, slot in enumerate((zs * 2 + 1 - y, zs * 2 + y)):
                forward(slot, pl.ds(c * piece, piece), 2 * i + k, c, True)
            pair_copy(i, c).wait_send()
            if i > 0:
                line_copy(i, c).wait_send()


def project_and_attend(sizes, tokens, norm_gain, layer, queries, key_cache, value_cache, lengths):
    grp, _, _ = sizes
    batch_rows, steps, width = tokens.shape
    _, slots, kv_width = key_cache.shape
    rows = batch_rows * steps
    depth, columns = layer.shape
    blocks, line = width // depth, grp // 2
    kv_heads, share = kv_width // HEAD_SIZE, queries.shape[2] // kv_width
    few = 128 // slots
    half = HEAD_SIZE // 2
    positions = (lengths[:, None] + jnp.arange(steps, dtype=jnp.int32)[None, :]).astype(jnp.float32)
    frequency = rope_base ** (-(jnp.arange(half, dtype=jnp.float32) * 2.0 / HEAD_SIZE))
    angles = positions.reshape(rows, 1) * frequency[None, :]
    cosine, sine = jnp.cos(angles), jnp.sin(angles)
    cosine = jnp.concatenate([cosine, cosine], axis=1)
    sine = jnp.concatenate([-sine, sine], axis=1)
    present = (jnp.arange(slots, dtype=jnp.int32)[None, :] < lengths[:, None]).astype(jnp.float32)
    present = present.reshape(batch_rows // few, few * slots)
    dma = pltpu.SemaphoreType.DMA
    vmem = pl.BlockSpec(memory_space=pltpu.VMEM)
    anywhere = pl.BlockSpec(memory_space=pl.ANY)
    flat_queries = queries.reshape(rows, queries.shape[2])
    part = pltpu.VMEM((batch_rows // few, kv_heads, share * few * steps, HEAD_SIZE), jnp.float32)
    attended, appended = pl.pallas_call(
        functools.partial(exchange_kernel, sizes),
        out_shape=(
            jax.ShapeDtypeStruct(flat_queries.shape, jnp.bfloat16),
            jax.ShapeDtypeStruct((rows, columns), jnp.bfloat16),
        ),
        in_specs=[vmem] * 6 + [anywhere] * 3,
        out_specs=(vmem, vmem),
        scratch_shapes=[
            pltpu.VMEM((blocks, rows, depth), jnp.bfloat16),
            pltpu.VMEM((grp, rows, depth), jnp.bfloat16),
            pltpu.VMEM((8, rows), jnp.float32),
            pltpu.VMEM((3, 8, rows), jnp.float32),
            pltpu.VMEM((line, rows, columns), jnp.bfloat16),
            pltpu.VMEM((line, rows, columns), jnp.bfloat16),
            pltpu.VMEM((line, rows, columns), jnp.float32),
            pltpu.VMEM((line, rows, columns), jnp.bfloat16),
            pltpu.VMEM((line, rows, columns), jnp.bfloat16),
            pltpu.VMEM(flat_queries.shape, jnp.bfloat16),
            pltpu.VMEM(key_cache.shape, jnp.bfloat16),
            pltpu.VMEM(value_cache.shape, jnp.bfloat16),
            part,
            part,
            part,
            dma((3,)),
            dma((3,)),
            dma((blocks, PIECES)),
            dma((grp, PIECES)),
            dma((grp, PIECES)),
            dma((grp, PIECES)),
            dma((line, PIECES)),
            dma((line, PIECES)),
            dma((line, PIECES)),
            dma((line, PIECES)),
            dma((3,)),
        ],
        compiler_params=pltpu.CompilerParams(collective_id=0, has_side_effects=True, vmem_limit_bytes=48 << 20),
    )(
        tokens.reshape(rows, width), norm_gain.reshape(1, width), layer, cosine, sine, present, flat_queries, key_cache,
        value_cache,
    )
    return attended.reshape(queries.shape), appended.reshape(batch_rows, steps, columns)


def fits(sizes, tokens, layer_half, queries, key_cache):
    grp, tp, fs = sizes
    batch_rows, steps, width = tokens.shape
    rows, depth, columns = batch_rows * steps, layer_half.shape[0], layer_half.shape[1]
    slots, kv_width = key_cache.shape[1:]
    if tp != 2 or fs != 2 or grp % 4 or not 4 <= grp <= 16 or 128 % slots or slots % 16:
        return False
    few = 128 // slots
    return (
        depth % 128 == 0 and width % depth == 0 and rows % 128 == 0 and rows % (16 * PIECES) == 0
        and columns == 2 * kv_width and few * steps % 16 == 0 and batch_rows % (few * PIECES) == 0
        and queries.shape[2] % kv_width == 0
    )


def project_gathered(tokens, norm_gain, layer_half):
    batch_rows, steps = (tokens.shape[0], tokens.shape[1])
    widened, gain_whole = (
        lax.all_gather(tokens, ("tp", "fs"), axis=2, tiled=True),
        lax.all_gather(norm_gain, ("tp", "fs"), axis=0, tiled=True),
    )
    mean_square = (
        jnp.einsum("rsd,rsd->rs", widened, widened, preferred_element_type=jnp.float32)[..., None]
        / MODEL_WIDTH
    )
    normed = (widened * lax.rsqrt(mean_square + norm_eps) * gain_whole.astype(jnp.float32)).astype(
        jnp.bfloat16
    )
    flattened = normed.reshape(batch_rows * steps, MODEL_WIDTH)
    gathered = lax.all_gather(layer_half, "grp", axis=0, tiled=True)
    return jnp.dot(flattened, gathered, preferred_element_type=jnp.float32)


def shards(
    sizes,
    tokens,
    norm_gain,
    queries,
    rotated_key_cache,
    head_value_cache,
    lengths,
    master,
    moment_first,
    moment_second,
    gradient,
):
    average = beta_first * moment_first + (1.0 - beta_first) * gradient
    variance = beta_second * moment_second + (1.0 - beta_second) * gradient * gradient
    update = average / correct_first / (jnp.sqrt(variance / correct_second) + adam_eps)
    renewed = master - learn_rate * (update + decay_rate * master)
    layer_half = renewed.astype(jnp.bfloat16)
    batch_rows, steps = (tokens.shape[0], tokens.shape[1])
    columns = layer_half.shape[1]
    if fits(sizes, tokens, layer_half, queries, rotated_key_cache):
        attended, appended = project_and_attend(
            sizes, tokens, norm_gain, layer_half, queries, rotated_key_cache, head_value_cache, lengths
        )
        return (attended, appended, renewed, average, variance)
    projected_output = project_gathered(tokens, norm_gain, layer_half)
    kv_heads = columns // (2 * HEAD_SIZE)
    projected_output = projected_output.reshape(batch_rows, steps, kv_heads, 2, HEAD_SIZE)
    positions = (lengths[:, None] + jnp.arange(steps, dtype=jnp.int32)[None, :]).astype(jnp.float32)
    key_new = rotate(projected_output[:, :, :, 0, :], positions).astype(jnp.bfloat16)
    value_new = projected_output[:, :, :, 1, :].astype(jnp.bfloat16)
    appended = jnp.stack([key_new, value_new], axis=3).reshape(batch_rows, steps, columns)
    attended = attention(queries, rotated_key_cache, head_value_cache, key_new, value_new, lengths)
    return (attended, appended, renewed, average, variance)


def solution(mesh):
    in_specs = (
        P("grp", None, ("tp", "fs")),
        P(("tp", "fs")),
        P("grp", None, ("tp", "fs")),
        P("grp", None, ("tp", "fs")),
        P("grp", None, ("tp", "fs")),
        P("grp"),
        P("grp", ("tp", "fs")),
        P("grp", ("tp", "fs")),
        P("grp", ("tp", "fs")),
        P("grp", ("tp", "fs")),
    )
    out_specs = (
        P("grp", None, ("tp", "fs")),
        P("grp", None, ("tp", "fs")),
        P("grp", ("tp", "fs")),
        P("grp", ("tp", "fs")),
        P("grp", ("tp", "fs")),
    )
    return jax.shard_map(
        functools.partial(shards, tuple(mesh.shape[name] for name in ("grp", "tp", "fs"))), mesh=mesh, in_specs=in_specs, out_specs=out_specs, check_vma=False,
    )
```
